512 devices in a mesh: ctx: 64 (over y_lo, z, x), head: 8 (over y_hi, core).
Axes of the slice: x: 4, y: 8 (y_hi: 4, y_lo: 2; y = y_hi * 2 + y_lo), z: 8, core: 2. Of those that a mesh axis runs over, the one named last changes fastest.
Arguments:
- queries: bfloat16 [8192, 8192], P('ctx', 'head'), may hold values from -15 to 15
- keys: bfloat16 [8192, 1024], P('ctx', 'head'), may hold values from -6 to 6
- values: bfloat16 [8192, 1024], P('ctx', 'head'), may hold values from -6 to 6
- window: int32 [8], P('head'), may hold values from 512 to 1024, as said below
Outputs:
- loss: float32 [], replicated
- grad_queries: float32 [8192, 8192], P('ctx', 'head')
- grad_keys: float32 [8192, 1024], P('ctx', 'head')
- grad_values: float32 [8192, 1024], P('ctx', 'head')
The draws below stay inside these ranges and needn't reach their ends.
Inputs may be any that keep to these rules, and one draw needn't show every extreme that they name: Some key-value head's window is exactly 1024.
All inputs are finite; a program needn't handle non-finite values.
Results may differ from the reference program's by a relative error of at most 0.0095.
Values may be sent and summed in bfloat16 or wider, within the bound.
No kernel may reach another device: no remote copies, remote signals or barrier semaphores. Data moves between devices by JAX's collectives and lax.ppermute only.
A program may use at most 64 MiB of HBM per device.

```python
import math
import jax
import jax.numpy as jnp
from jax import lax

QH = 64
KVH = 8
HD = 128
WINDOW = 1024
SEQ = 8192


def query_key_pair(key):
    base_key = jax.random.fold_in(key, 11)
    key_q, key_k = jax.random.split(base_key, 2)
    query_part = 2.5 * jnp.clip(jax.random.normal(key_q, (SEQ, QH * HD), jnp.float32), -6.0, 6.0)
    key_part = jnp.clip(jax.random.normal(key_k, (SEQ, KVH * HD), jnp.float32), -6.0, 6.0)
    return (query_part, key_part)


def draw_queries(key, part):
    return query_key_pair(key)[0].astype(jnp.bfloat16)


def draw_keys(key, part):
    return query_key_pair(key)[1].astype(jnp.bfloat16)


def draw_window(key, part):
    lengths = jax.random.randint(jax.random.fold_in(key, 5), (KVH,), WINDOW // 2, WINDOW + 1)
    chosen = jax.random.randint(jax.random.fold_in(key, 6), (), 0, KVH)
    return jnp.where(jnp.arange(KVH) == chosen, WINDOW, lengths).astype(jnp.int32)


def block_levels(key, shape, shards, smallest, largest):
    def one(axis_at, parts):
        steps = jax.random.uniform(jax.random.fold_in(jax.random.fold_in(key, 6), axis_at), (parts,), jnp.float32, smallest / len(shards), largest / len(shards))
        return jnp.repeat(jnp.exp(steps), shape[axis_at] // parts).reshape((-1,) + (1,) * (len(shape) - axis_at - 1))

    factor_of = one(*shards[0])
    for cut in shards[1:]:
        factor_of = factor_of * one(*cut)
    return factor_of


def normal_values(key, shape, scale, reach, pieces=(), kind=jnp.bfloat16):
    drawn = jax.random.normal(key, shape, jnp.float32) * scale
    if len(pieces) > 0:
        drawn = block_levels(key, shape, pieces, -0.22, 0.18) * drawn
    return jnp.clip(drawn, min=-reach, max=reach).astype(kind)


def setup_inputs(seed: int = 0) -> dict:
    streams_of = jax.random.split(jax.random.key(seed), 5)
    queries = draw_queries(jax.random.fold_in(streams_of[4], 71), 0)
    keys = draw_keys(jax.random.fold_in(streams_of[4], 71), 0)
    values = normal_values(streams_of[2], (SEQ, KVH * HD), 1.0, 6.0, ((0, 64), (1, 8)))
    window = draw_window(jax.random.fold_in(streams_of[4], 71), 0)
    return {"queries": queries, "keys": keys, "values": values, "window": window}


masked_score = -1e+30

def rounded(values_in):
    return lax.optimization_barrier(values_in.astype(jnp.bfloat16)).astype(jnp.float32)

def one_group(operands):
    group_q, group_k, group_v, group_w = operands
    block_rows = math.gcd(512, SEQ)
    inverse_root = 1.0 / math.sqrt(HD)
    query_f = group_q.astype(jnp.float32)
    keys_f = group_k.astype(jnp.float32)
    values_f = group_v.astype(jnp.float32)
    positions = jnp.arange(SEQ, dtype=jnp.int32)
    grad_keys = jnp.zeros((SEQ, HD), jnp.float32)
    grad_values = jnp.zeros((SEQ, HD), jnp.float32)
    grad_rows = []
    square_sum = jnp.zeros((), jnp.float32)
    for block_index in range(SEQ // block_rows):
        low_row = block_index * block_rows
        high_row = low_row + block_rows
        start_key = max(0, low_row - WINDOW)
        query_block = query_f[low_row:high_row]
        query_pos = positions[low_row:high_row]
        key_pos = positions[:high_row]
        visible = key_pos[None, :] <= query_pos[:, None]
        scores = jnp.einsum('tgd,sd->gts', query_block, keys_f[:high_row]) * inverse_root
        scores = jnp.where(visible[None], scores, masked_score)
        exponent = jnp.where(visible[None], jnp.exp(scores - lax.optimization_barrier(jnp.max(scores, axis=-1, keepdims=True))), 0.0)
        teacher_sum = jnp.einsum('gts,sd->tgd', rounded(exponent), values_f[:high_row])
        teacher_out = rounded(teacher_sum / lax.optimization_barrier(jnp.sum(exponent, axis=-1)).T[..., None])
        near_pos = positions[start_key:high_row]
        allowed = (near_pos[None, :] <= query_pos[:, None]) & (near_pos[None, :] > query_pos[:, None] - group_w)
        near_keys = keys_f[start_key:high_row]
        near_values = values_f[start_key:high_row]
        scores = jnp.einsum('tgd,sd->gts', query_block, near_keys) * inverse_root
        scores = jnp.where(allowed[None], scores, masked_score)
        exponent = jnp.where(allowed[None], jnp.exp(scores - lax.optimization_barrier(jnp.max(scores, axis=-1, keepdims=True))), 0.0)
        totals = lax.optimization_barrier(jnp.sum(exponent, axis=-1))
        student_out = jnp.einsum('gts,sd->tgd', rounded(exponent), near_values) / totals.T[..., None]
        difference = student_out - teacher_out
        square_sum = square_sum + jnp.sum(difference * difference)
        grad_out = rounded(difference)
        probabilities = exponent / totals[..., None]
        grad_values = grad_values.at[start_key:high_row].add(jnp.einsum('gts,tgd->sd', rounded(probabilities), grad_out))
        row_dot = lax.optimization_barrier(jnp.sum(difference * student_out, axis=-1))
        grad_probs = jnp.einsum('tgd,sd->gts', grad_out, near_values)
        grad_scores = rounded(probabilities * (grad_probs - row_dot.T[..., None]))
        grad_rows.append(jnp.einsum('gts,sd->tgd', grad_scores, near_keys) * inverse_root)
        grad_keys = grad_keys.at[start_key:high_row].add(jnp.einsum('gts,tgd->sd', grad_scores, query_block) * inverse_root)
    return (jnp.concatenate(grad_rows, axis=0), grad_keys, grad_values, square_sum)

def reference(queries, keys, values, window):
    group_size = QH // KVH
    grouped_q = queries.reshape(SEQ, KVH, group_size, HD).transpose(1, 0, 2, 3)
    grouped_k = keys.reshape(SEQ, KVH, HD).transpose(1, 0, 2)
    grouped_v = values.reshape(SEQ, KVH, HD).transpose(1, 0, 2)
    grad_q, grad_k, grad_v, squares = lax.map(one_group, (grouped_q, grouped_k, grouped_v, window))
    loss = jnp.sum(squares) / (SEQ * QH * HD)
    return (loss, grad_q.transpose(1, 0, 2, 3).reshape(SEQ, QH * HD), grad_k.transpose(1, 0, 2).reshape(SEQ, KVH * HD), grad_v.transpose(1, 0, 2).reshape(SEQ, KVH * HD))
```

```python
import functools
import math

import jax
import jax.numpy as jnp
from jax import lax
from jax.experimental import pallas as pl
from jax.experimental.pallas import tpu as pltpu
from jax.sharding import Mesh
from jax.sharding import PartitionSpec as P

QH = 64
KVH = 8
HD = 128
SEQ = 8192
GROUP = QH // KVH
BLK = 128
WSPAN = 8
X = 4
ROWS = 16
CHUNK = 4
TILE = 256
WIN = (WSPAN + 1) * BLK
SLOTS = 12
OROWS = GROUP * BLK + 32
TROWS = 3 * 2 * HD + 32

CTX = ("y", "z", "x")
HEAD = ("yh", "core")
ROW = ("y", "z")

SCALE = 1.0 / math.sqrt(HD)
SCALE2 = SCALE * math.log2(math.e)
NEG = -1e30


def dot(a, b):
    return lax.dot_general(a, b, (((1,), (0,)), ((), ())), preferred_element_type=jnp.float32)


def dot_t(a, b):
    return lax.dot_general(a, b, (((1,), (1,)), ((), ())), preferred_element_type=jnp.float32)


def three_terms(value):
    high = value.astype(jnp.bfloat16)
    rest = value - high.astype(jnp.float32)
    middle = rest.astype(jnp.bfloat16)
    low = (rest - middle.astype(jnp.float32)).astype(jnp.bfloat16)
    f = jnp.float32
    first = jnp.concatenate([high.astype(f), middle.astype(f)], axis=0).astype(jnp.bfloat16)
    second = jnp.concatenate([low.astype(f), jnp.zeros_like(value)], axis=0).astype(jnp.bfloat16)
    return first, second


def from_terms(first, second):
    a = first.astype(jnp.float32)
    b = second.astype(jnp.float32)
    return a[0:8] + a[8:16] + b[0:8]


def head_pair(ref_block, pair):
    low = ref_block[:, pl.ds(pl.multiple_of(pair * 2 * HD, 2 * HD), HD)]
    high = ref_block[:, pl.ds(pl.multiple_of(pair * 2 * HD + HD, HD), HD)]
    return jnp.concatenate([low, high], axis=0)


def teacher_kernel(place, q_ref, kv_ref, o_ref, vext, lse_ref):
    row = place[0]
    mine = place[1]
    vext[:, :, 0:HD] = kv_ref[:, :, HD : 2 * HD]
    vext[:, :, HD : 2 * HD] = jnp.ones((ROWS, BLK, HD), jnp.bfloat16)
    full = row // CHUNK
    width = CHUNK * BLK

    def tile(step, carry):
        block = step // 4
        pair = step % 4
        q = head_pair(q_ref.at[block], pair)

        def visit(chunk, state, masked):
            top, acc = state
            start = pl.multiple_of(chunk * CHUNK, CHUNK)
            k = kv_ref[pl.ds(start, CHUNK), :, 0:HD].reshape(width, HD)
            v = vext[pl.ds(start, CHUNK), :, :].reshape(width, 2 * HD)
            s = dot_t(q, k)
            if masked:
                token = lax.broadcasted_iota(jnp.int32, (TILE, 1), 0) % BLK
                reach = jnp.where(mine < block, BLK - 1, jnp.where(mine == block, token, -1))
                limit = (row - start) * BLK + reach
                column = lax.broadcasted_iota(jnp.int32, (TILE, width), 1)
                s = jnp.where(column <= limit, s, NEG)
            new_top = jnp.maximum(top, jnp.max(s, axis=1, keepdims=True))
            p = jnp.exp2(s * SCALE2 - new_top * SCALE2)
            factor = jnp.exp2((top - new_top) * SCALE2)
            acc = acc * factor + dot(p.astype(jnp.bfloat16), v)
            return new_top, acc

        state = (jnp.full((TILE, 1), NEG, jnp.float32), jnp.zeros((TILE, 2 * HD), jnp.float32))
        state = lax.fori_loop(0, full, lambda c, st: visit(c, st, False), state)
        top, acc = visit(full, state, True)
        total = acc[:, HD:]
        out = (acc[:, 0:HD] / total).astype(jnp.bfloat16)
        o_ref[block, pl.ds(pl.multiple_of(pair * TILE, TILE), TILE), :] = out
        lse = (top * SCALE2 + jnp.log2(total)).T
        lse_ref[block, pl.ds(pair * 2, 1), :] = lse[0:1, 0:BLK]
        lse_ref[block, pl.ds(pair * 2 + 1, 1), :] = lse[0:1, BLK : 2 * BLK]
        return carry

    lax.fori_loop(0, X * 4, tile, 0)
    for block in range(X):
        first, second = three_terms(lse_ref[block])
        o_ref[block, GROUP * BLK : GROUP * BLK + 16, :] = first
        o_ref[block, GROUP * BLK + 16 : OROWS, :] = second


def teacher_parts(place, queries, kv):
    return pl.pallas_call(
        teacher_kernel,
        out_shape=jax.ShapeDtypeStruct((X, OROWS, HD), jnp.bfloat16),
        in_specs=[
            pl.BlockSpec(memory_space=pltpu.SMEM),
            pl.BlockSpec(memory_space=pltpu.VMEM),
            pl.BlockSpec(memory_space=pltpu.VMEM),
        ],
        out_specs=pl.BlockSpec(memory_space=pltpu.VMEM),
        scratch_shapes=[
            pltpu.VMEM((ROWS, BLK, 2 * HD), jnp.bfloat16),
            pltpu.VMEM((X, 8, BLK), jnp.float32),
        ],
        name="teacher",
    )(place, queries, kv)


def student_kernel(
    place, q_ref, near_ref, part_ref, dq_ref, term_ref, kw, vw, dkt, dvt, weight_ref, square_ref
):
    mine = place[1]
    block = place[2]
    window = place[3]
    for j in range(WSPAN + 1):
        slot = mine + j
        source = slot % X
        column = pl.multiple_of((slot // X) * 2 * HD, 2 * HD)
        kw[j * BLK : (j + 1) * BLK, :] = near_ref[source, :, pl.ds(column, HD)]
        vw[j * BLK : (j + 1) * BLK, :] = near_ref[source, :, pl.ds(column + HD, HD)]
    dkt[...] = jnp.zeros_like(dkt)
    dvt[...] = jnp.zeros_like(dvt)
    square_ref[...] = jnp.zeros_like(square_ref)

    lse = [
        from_terms(
            part_ref[k, GROUP * BLK : GROUP * BLK + 16, :],
            part_ref[k, GROUP * BLK + 16 : OROWS, :],
        )
        for k in range(X)
    ]
    top = functools.reduce(jnp.maximum, lse)
    shares = [jnp.exp2(v - top) for v in lse]
    total = shares[0] + shares[1] + shares[2] + shares[3]
    for k in range(X):
        weight_ref[k] = shares[k] / total

    def tile(pair, carry):
        q = head_pair(q_ref, pair)
        token = lax.broadcasted_iota(jnp.int32, (TILE, 1), 0) % BLK
        last = WSPAN * BLK + token
        first = jnp.maximum(last - window + 1, (WSPAN - block) * BLK)
        column = lax.broadcasted_iota(jnp.int32, (TILE, WIN), 1)
        visible = (column >= first) & (column <= last)
        s = jnp.where(visible, dot_t(q, kw[...]), NEG)
        peak = jnp.max(s, axis=1, keepdims=True)
        p = jnp.exp2(s * SCALE2 - peak * SCALE2)
        inverse = 1.0 / jnp.sum(p, axis=1, keepdims=True)
        student = dot(p.astype(jnp.bfloat16), vw[...]) * inverse

        teacher = jnp.zeros((TILE, HD), jnp.float32)
        for k in range(X):
            low = jnp.broadcast_to(weight_ref[k, pl.ds(pair * 2, 1), :], (HD, BLK)).T
            high = jnp.broadcast_to(weight_ref[k, pl.ds(pair * 2 + 1, 1), :], (HD, BLK)).T
            weight = jnp.concatenate([low, high], axis=0)
            part = part_ref[k, pl.ds(pl.multiple_of(pair * TILE, TILE), TILE), :]
            teacher = teacher + weight * part.astype(jnp.float32)
        difference = student - teacher.astype(jnp.bfloat16).astype(jnp.float32)
        square_ref[...] += jnp.sum((difference * difference).reshape(TILE // 8, 8, HD), axis=0)
        grad_out = difference.astype(jnp.bfloat16)
        row_dot = jnp.sum(difference * student, axis=1, keepdims=True)

        prob = p * inverse
        dvt[...] += dot(grad_out.T, prob.astype(jnp.bfloat16))
        grad_p = dot_t(grad_out, vw[...])
        grad_s = (prob * (grad_p - row_dot)).astype(jnp.bfloat16)
        dkt[...] += dot(q.T, grad_s)
        dq = dot(grad_s, kw[...]) * SCALE
        dq_ref[:, pl.ds(pl.multiple_of(pair * 2 * HD, 2 * HD), HD)] = dq[0:BLK]
        dq_ref[:, pl.ds(pl.multiple_of(pair * 2 * HD + HD, HD), HD)] = dq[BLK:]
        return carry

    lax.fori_loop(0, 4, tile, 0)
    term_ref[...] = jnp.zeros_like(term_ref)
    for j in range(WSPAN + 1):
        slot = mine + j
        source = slot % X
        at = pl.multiple_of((slot // X) * 2 * HD, 2 * HD)
        cols = slice(j * BLK, (j + 1) * BLK)
        term_ref[source, pl.ds(at, HD), :] = dkt[:, cols].astype(jnp.bfloat16)
        term_ref[source, pl.ds(at + HD, HD), :] = dvt[:, cols].astype(jnp.bfloat16)
    squares = jnp.broadcast_to(jnp.sum(square_ref[...], keepdims=True), (8, BLK))
    one, two = three_terms(squares)
    for k in range(X):
        term_ref[k, TROWS - 32 : TROWS - 16, :] = one
        term_ref[k, TROWS - 16 : TROWS, :] = two


def student_step(place, queries, near, parts):
    vmem = pl.BlockSpec(memory_space=pltpu.VMEM)
    return pl.pallas_call(
        student_kernel,
        out_shape=(
            jax.ShapeDtypeStruct((BLK, GROUP * HD), jnp.float32),
            jax.ShapeDtypeStruct((X, TROWS, BLK), jnp.bfloat16),
        ),
        in_specs=[pl.BlockSpec(memory_space=pltpu.SMEM), vmem, vmem, vmem],
        out_specs=(vmem, vmem),
        scratch_shapes=[
            pltpu.VMEM((WIN, HD), jnp.bfloat16),
            pltpu.VMEM((WIN, HD), jnp.bfloat16),
            pltpu.VMEM((HD, WIN), jnp.float32),
            pltpu.VMEM((HD, WIN), jnp.float32),
            pltpu.VMEM((X, 8, BLK), jnp.float32),
            pltpu.VMEM((8, HD), jnp.float32),
        ],
        name="student",
    )(place, queries, near, parts)


def to_all(value, axes, count):
    spread = jnp.broadcast_to(value[None], (count,) + value.shape)
    return lax.all_to_all(spread, axes, 0, 0, tiled=True)


def body(queries, keys, values, window):
    row = lax.axis_index(ROW)
    mine = lax.axis_index("x")
    block = row * X + mine
    place = jnp.stack([row, mine, block, window[0]]).astype(jnp.int32)

    kv = to_all(jnp.concatenate([keys, values], axis=1), ROW, ROWS)
    before = [
        lax.dynamic_index_in_dim(kv, jnp.maximum(row - 2 + k, 0), 0, keepdims=False)
        for k in range(3)
    ]
    sent = jnp.concatenate([queries] + before, axis=1)
    around = to_all(sent, "x", X)
    all_q = around[:, :, : GROUP * HD]
    near = around[:, :, GROUP * HD :]

    parts = teacher_parts(place, all_q, kv)
    parts = lax.all_to_all(parts, "x", 0, 0, tiled=True)
    grad_q, terms = student_step(place, queries, near, parts)
    terms = lax.all_to_all(terms, "x", 0, 0, tiled=True)

    summed = jnp.sum(terms.astype(jnp.float32), axis=0)
    sums = summed[: TROWS - 32].reshape(3, 2 * HD, BLK)
    piece = summed[TROWS - 32 :]
    squares = piece[0:8] + piece[8:16] + piece[16:24]

    def back(value, steps):
        return lax.ppermute(
            value.astype(jnp.bfloat16), ROW, [(r, r - steps) for r in range(steps, ROWS)]
        )

    one = back(sums[1], 1)
    two = back(sums[0], 2)
    grads = sums[2] + one.astype(jnp.float32) + two.astype(jnp.float32)
    grad_k = grads[:HD].T * SCALE
    grad_v = grads[HD:].T

    squares = jnp.sum(to_all(squares, ("y", "z", "core"), 32), axis=0)
    squares = jnp.sum(to_all(squares, "yh", 4), axis=0)
    loss = squares[0, 0] / (SEQ * QH * HD)
    return (loss, grad_q, grad_k, grad_v)


def solution(mesh):
    finer = Mesh(mesh.devices.reshape(2, 8, 4, 4, 2), ("y", "z", "x", "yh", "core"))
    return jax.shard_map(
        body,
        mesh=finer,
        in_specs=(P(CTX, HEAD), P(CTX, HEAD), P(CTX, HEAD), P(HEAD)),
        out_specs=(P(), P(CTX, HEAD), P(CTX, HEAD), P(CTX, HEAD)),
        check_vma=False,
    )
```

```python
import functools
import math

import jax
import jax.numpy as jnp
from jax import lax
from jax.experimental import pallas as pl
from jax.experimental.pallas import tpu as pltpu
from jax.sharding import Mesh
from jax.sharding import PartitionSpec as P

QH = 64
KVH = 8
HD = 128
SEQ = 8192
GROUP = QH // KVH
BLK = 128
WSPAN = 8
X = 4
ROWS = 16
PLANE = 8
TILE = 256
TILES = X * GROUP * BLK // TILE
WIN = (WSPAN + 1) * BLK
OROWS = GROUP * BLK + 32
TROWS = 3 * 2 * HD


CTX = ("y", "z", "x")
HEAD = ("yh", "core")
ROW = ("y", "z")

SCALE = 1.0 / math.sqrt(HD)
SCALE2 = SCALE * math.log2(math.e)
NEG = -1e30


def dot(a, b):
    return lax.dot_general(a, b, (((1,), (0,)), ((), ())), preferred_element_type=jnp.float32)


def three_terms(value):
    high = value.astype(jnp.bfloat16)
    rest = value - high.astype(jnp.float32)
    middle = rest.astype(jnp.bfloat16)
    low = (rest - middle.astype(jnp.float32)).astype(jnp.bfloat16)
    f = jnp.float32
    first = jnp.concatenate([high.astype(f), middle.astype(f)], axis=0).astype(jnp.bfloat16)
    second = jnp.concatenate([low.astype(f), jnp.zeros_like(value)], axis=0).astype(jnp.bfloat16)
    return first, second


def from_terms(first, second):
    a = first.astype(jnp.float32)
    b = second.astype(jnp.float32)
    return a[0:8] + a[8:16] + b[0:8]


def head_pair(ref_block, pair):
    low = ref_block[:, pl.ds(pl.multiple_of(pair * 2 * HD, 2 * HD), HD)]
    high = ref_block[:, pl.ds(pl.multiple_of(pair * 2 * HD + HD, HD), HD)]
    return jnp.concatenate([low, high], axis=0)


def token_of_lane(shape):
    return lax.broadcasted_iota(jnp.int32, shape, 1) % BLK


def gather_queries(q_all, q_refs, mine):
    for shift, q_ref in enumerate(q_refs):
        source = (mine + X - shift) % X
        for g in range(GROUP):
            lanes = slice((g % 2) * BLK, (g % 2 + 1) * BLK)
            q_all[source * 4 + g // 2, :, lanes] = q_ref[g * HD : (g + 1) * HD, :]


def gather_values(vt, kv_ref):
    for b in range(PLANE):
        vt[0:HD, b * BLK : (b + 1) * BLK] = kv_ref[b, HD : 2 * HD, :]
    vt[HD:, :] = jnp.ones((16, PLANE * BLK), jnp.bfloat16)


def score_and_sum(q, kv_ref, vt, top_of_last, write, read, limit):
    p = jnp.exp2(read[...] * SCALE2 - top_of_last)
    acc = dot(vt[...], p.astype(jnp.bfloat16))
    if write is None:
        return None, acc
    s = dot(kv_ref[:, 0:HD, :].reshape(PLANE * BLK, HD), q)
    if limit is not None:
        s = jnp.where(lax.broadcasted_iota(jnp.int32, s.shape, 0) <= limit, s, NEG)
    write[...] = s
    return jnp.max(s, axis=0, keepdims=True) * SCALE2, acc


def own_plane_kernel(
    place, q0, q1, q2, q3, kv_ref, acc_ref, top_ref, q_ref, vt, held_a, held_b
):
    mine = place[1]
    in_plane = place[4]
    gather_queries(q_ref, (q0, q1, q2, q3), mine)
    gather_values(vt, kv_ref)

    def tile(step, top_of_last, write, read):
        ahead = jnp.minimum(step, TILES - 1)
        block = ahead // 4
        reach = jnp.where(
            mine < block, BLK - 1, jnp.where(mine == block, token_of_lane((1, TILE)), -1)
        )
        top, acc = score_and_sum(
            q_ref[ahead], kv_ref, vt, top_of_last, write, read, in_plane * BLK + reach
        )
        done = jnp.maximum(step - 1, 0)
        acc_ref[done] = acc
        top_ref[done] = jnp.broadcast_to(top_of_last, (8, TILE))
        return top

    def two_tiles(step, top):
        top = tile(step * 2, top, held_a, held_b)
        return tile(step * 2 + 1, top, held_b, held_a)

    top = lax.fori_loop(0, TILES // 2, two_tiles, jnp.zeros((1, TILE), jnp.float32))
    tile(TILES, top, None, held_b)


def own_plane(place, queries, kv):
    vmem = pl.BlockSpec(memory_space=pltpu.VMEM)
    return pl.pallas_call(
        own_plane_kernel,
        out_shape=(
            jax.ShapeDtypeStruct((TILES, HD + 16, TILE), jnp.float32),
            jax.ShapeDtypeStruct((TILES, 8, TILE), jnp.float32),
            jax.ShapeDtypeStruct((TILES, HD, TILE), jnp.bfloat16),
        ),
        in_specs=[pl.BlockSpec(memory_space=pltpu.SMEM)] + [vmem] * 5,
        out_specs=(vmem, vmem, vmem),
        scratch_shapes=[
            pltpu.VMEM((HD + 16, PLANE * BLK), jnp.bfloat16),
            pltpu.VMEM((PLANE * BLK, TILE), jnp.float32),
            pltpu.VMEM((PLANE * BLK, TILE), jnp.float32),
        ],
        cost_estimate=pl.CostEstimate(
            flops=4 * 4096 * 1024 * 128, bytes_accessed=3_000_000, transcendentals=4096 * 1024
        ),
        name="own_plane",
    )(place, *queries, kv)


def other_plane_kernel(
    place, q_ref, acc_ref, top_ref, kv_ref, o_ref, vt, held_a, held_b, lse_ref, extra
):
    upper = place[5]
    gather_values(vt, kv_ref)
    extra[...] = jnp.zeros_like(extra)

    def tile(step, top_of_last, write, read):
        ahead = jnp.minimum(step, TILES - 1)

        def visit(_, top):
            top, acc = score_and_sum(q_ref[ahead], kv_ref, vt, top_of_last, write, read, None)
            extra[...] = acc
            return jnp.full((1, TILE), NEG, jnp.float32) if top is None else top

        top = lax.fori_loop(0, upper, visit, jnp.full((1, TILE), NEG, jnp.float32))

        done = jnp.maximum(step - 1, 0)
        first_top = top_ref[done, 0:1, :]
        joint = jnp.maximum(first_top, top_of_last)
        scale_first = jnp.exp2(first_top - joint)
        scale_second = jnp.exp2(top_of_last - joint)
        total = (
            acc_ref[done, HD : HD + 1, :] * scale_first + extra[HD : HD + 1, :] * scale_second
        )
        inverse = 1.0 / total
        out = (
            acc_ref[done, 0:HD, :] * (scale_first * inverse)
            + extra[0:HD, :] * (scale_second * inverse)
        ).astype(jnp.bfloat16)
        lse = joint + jnp.log2(total)
        block, pair = done // 4, done % 4
        o_ref[block, pl.ds(pl.multiple_of(pair * TILE, TILE), HD), :] = out[:, 0:BLK]
        o_ref[block, pl.ds(pl.multiple_of(pair * TILE + HD, HD), HD), :] = out[:, BLK:]
        lse_ref[block, pl.ds(pair * 2, 1), :] = lse[:, 0:BLK]
        lse_ref[block, pl.ds(pair * 2 + 1, 1), :] = lse[:, BLK:]
        return top

    def two_tiles(step, top):
        top = tile(step * 2, top, held_a, held_b)
        return tile(step * 2 + 1, top, held_b, held_a)

    top = lax.fori_loop(0, TILES // 2, two_tiles, jnp.full((1, TILE), NEG, jnp.float32))
    tile(TILES, top, None, held_b)
    for block in range(X):
        first, second = three_terms(lse_ref[block])
        o_ref[block, GROUP * BLK : GROUP * BLK + 16, :] = first
        o_ref[block, GROUP * BLK + 16 : OROWS, :] = second


def other_plane(place, q_all, acc, top, kv):
    vmem = pl.BlockSpec(memory_space=pltpu.VMEM)
    return pl.pallas_call(
        other_plane_kernel,
        out_shape=jax.ShapeDtypeStruct((X, OROWS, HD), jnp.bfloat16),
        in_specs=[pl.BlockSpec(memory_space=pltpu.SMEM)] + [vmem] * 4,
        out_specs=vmem,
        scratch_shapes=[
            pltpu.VMEM((HD + 16, PLANE * BLK), jnp.bfloat16),
            pltpu.VMEM((PLANE * BLK, TILE), jnp.float32),
            pltpu.VMEM((PLANE * BLK, TILE), jnp.float32),
            pltpu.VMEM((X, 8, BLK), jnp.float32),
            pltpu.VMEM((HD + 16, TILE), jnp.float32),
        ],
        cost_estimate=pl.CostEstimate(
            flops=4 * 4096 * 1024 * 128, bytes_accessed=3_000_000, transcendentals=4096 * 1024
        ),
        name="other_plane",
    )(place, q_all, acc, top, kv)


def forward_kernel(place, q_ref, near_ref, prob_ref, out_ref, kt, vw, kw, vt):
    mine = place[1]
    block = place[2]
    window = place[3]
    for j in range(WSPAN + 1):
        slot = mine + j
        source = slot % X
        at = pl.multiple_of((slot // X) * 2 * HD, 2 * HD)
        here = slice(j * BLK, (j + 1) * BLK)
        k = near_ref[source, pl.ds(at, HD), :]
        v_t = near_ref[source, pl.ds(at + HD, HD), :]
        kw[here, :] = k
        kt[:, here] = k.T
        vw[here, :] = v_t.T
        vt[:, here] = v_t

    def tile(pair, carry):
        low = q_ref[pl.ds(pl.multiple_of(pair * TILE, TILE), HD), :]
        high = q_ref[pl.ds(pl.multiple_of(pair * TILE + HD, HD), HD), :]
        q = jnp.concatenate([low, high], axis=1)
        last = WSPAN * BLK + token_of_lane((1, TILE))
        first = jnp.maximum(last - window + 1, (WSPAN - block) * BLK)
        key = lax.broadcasted_iota(jnp.int32, (WIN, TILE), 0)
        s = jnp.where((key >= first) & (key <= last), dot(kw[...], q), NEG)
        peak = jnp.max(s, axis=0, keepdims=True) * SCALE2
        p = jnp.exp2(s * SCALE2 - peak)
        inverse = 1.0 / jnp.sum(p, axis=0, keepdims=True)
        out = dot(vt[...], p.astype(jnp.bfloat16)) * inverse
        at = pl.multiple_of(pair * TILE, TILE)
        prob_ref[:, pl.ds(at, TILE)] = (p * inverse).astype(jnp.bfloat16)
        out_ref[:, pl.ds(at, TILE)] = out
        return carry

    lax.fori_loop(0, 4, tile, 0)


def student_forward(place, queries, near):
    vmem = pl.BlockSpec(memory_space=pltpu.VMEM)
    return pl.pallas_call(
        forward_kernel,
        out_shape=(
            jax.ShapeDtypeStruct((WIN, GROUP * BLK), jnp.bfloat16),
            jax.ShapeDtypeStruct((HD, GROUP * BLK), jnp.float32),
            jax.ShapeDtypeStruct((HD, WIN), jnp.bfloat16),
            jax.ShapeDtypeStruct((WIN, HD), jnp.bfloat16),
        ),
        in_specs=[pl.BlockSpec(memory_space=pltpu.SMEM), vmem, vmem],
        out_specs=(vmem, vmem, vmem, vmem),
        scratch_shapes=[
            pltpu.VMEM((WIN, HD), jnp.bfloat16),
            pltpu.VMEM((HD, WIN), jnp.bfloat16),
        ],
        cost_estimate=pl.CostEstimate(
            flops=4 * 1024 * WIN * 128, bytes_accessed=4_000_000, transcendentals=1024 * WIN
        ),
        name="forward",
    )(place, queries, near)


def merge_kernel(part_ref, out_ref, grad_ref, dot_ref, square_ref, weight_ref, sq_ref):
    lse = [
        from_terms(
            part_ref[k, GROUP * BLK : GROUP * BLK + 16, :],
            part_ref[k, GROUP * BLK + 16 : OROWS, :],
        )
        for k in range(X)
    ]
    top = functools.reduce(jnp.maximum, lse)
    shares = [jnp.exp2(v - top) for v in lse]
    total = shares[0] + shares[1] + shares[2] + shares[3]
    for k in range(X):
        weight_ref[k] = shares[k] / total
    sq_ref[...] = jnp.zeros_like(sq_ref)
    for g in range(GROUP):
        rows = slice(g * HD, (g + 1) * HD)
        merged = jnp.zeros((HD, BLK), jnp.float32)
        for k in range(X):
            merged = merged + weight_ref[k, g : g + 1, :] * part_ref[k, rows, :].astype(jnp.float32)
        teacher = merged.astype(jnp.bfloat16).astype(jnp.float32)
        student = out_ref[:, rows]
        difference = student - teacher
        sq_ref[...] += jnp.sum((difference * difference).reshape(HD // 8, 8, BLK), axis=0)
        grad_ref[:, rows] = difference.astype(jnp.bfloat16)
        dot_ref[:, rows] = jnp.broadcast_to(
            jnp.sum(difference * student, axis=0, keepdims=True), (8, BLK)
        )
    square_ref[...] = jnp.broadcast_to(jnp.sum(sq_ref[...], keepdims=True), square_ref.shape)


def merge(parts, out):
    vmem = pl.BlockSpec(memory_space=pltpu.VMEM)
    return pl.pallas_call(
        merge_kernel,
        out_shape=(
            jax.ShapeDtypeStruct((HD, GROUP * BLK), jnp.bfloat16),
            jax.ShapeDtypeStruct((8, GROUP * BLK), jnp.float32),
            jax.ShapeDtypeStruct((X * GROUP, 8, BLK), jnp.float32),
        ),
        in_specs=[vmem, vmem],
        out_specs=(vmem, vmem, vmem),
        scratch_shapes=[
            pltpu.VMEM((X, 8, BLK), jnp.float32),
            pltpu.VMEM((8, BLK), jnp.float32),
        ],
        cost_estimate=pl.CostEstimate(flops=2_000_000, bytes_accessed=2_000_000, transcendentals=0),
        name="merge",
    )(parts, out)


def backward_kernel(place, q_ref, prob_ref, grad_ref, dot_ref, kt, vw, dq_ref, term_ref, dk, dv):
    mine = place[1]
    dk[...] = jnp.zeros_like(dk)
    dv[...] = jnp.zeros_like(dv)

    def tile(pair, carry):
        q = head_pair(q_ref, pair)
        at = pl.ds(pl.multiple_of(pair * TILE, TILE), TILE)
        grad_t = grad_ref[:, at]
        prob = prob_ref[:, at]
        grad_p = dot(vw[...], grad_t)
        grad_s = (prob.astype(jnp.float32) * (grad_p - dot_ref[0:1, at])).astype(jnp.bfloat16)
        dv[...] += dot(prob, grad_t.T)
        dk[...] += dot(grad_s, q)
        dq = (dot(kt[...], grad_s) * SCALE).T
        dq_ref[:, pl.ds(pl.multiple_of(pair * 2 * HD, 2 * HD), HD)] = dq[0:BLK]
        dq_ref[:, pl.ds(pl.multiple_of(pair * 2 * HD + HD, HD), HD)] = dq[BLK:]
        return carry

    lax.fori_loop(0, 4, tile, 0)
    term_ref[...] = jnp.zeros_like(term_ref)
    for j in range(WSPAN + 1):
        slot = mine + j
        source = slot % X
        at = pl.multiple_of((slot // X) * 2 * HD, 2 * HD)
        here = slice(j * BLK, (j + 1) * BLK)
        term_ref[source, pl.ds(at, HD), :] = dk[here, :].astype(jnp.bfloat16)
        term_ref[source, pl.ds(at + HD, HD), :] = dv[here, :].astype(jnp.bfloat16)


def student_backward(place, queries, prob, grad, row_dot, kt, vw):
    vmem = pl.BlockSpec(memory_space=pltpu.VMEM)
    return pl.pallas_call(
        backward_kernel,
        out_shape=(
            jax.ShapeDtypeStruct((BLK, GROUP * HD), jnp.float32),
            jax.ShapeDtypeStruct((X, TROWS, BLK), jnp.bfloat16),
        ),
        in_specs=[pl.BlockSpec(memory_space=pltpu.SMEM)] + [vmem] * 6,
        out_specs=(vmem, vmem),
        scratch_shapes=[
            pltpu.VMEM((WIN, HD), jnp.float32),
            pltpu.VMEM((WIN, HD), jnp.float32),
        ],
        cost_estimate=pl.CostEstimate(
            flops=10 * 1024 * WIN * 128, bytes_accessed=5_000_000, transcendentals=0
        ),
        name="backward",
    )(place, queries, prob, grad, row_dot, kt, vw)


def to_all(value, axes, count):
    spread = jnp.broadcast_to(value[None], (count,) + value.shape)
    return lax.all_to_all(spread, axes, 0, 0, tiled=True)


def step(queries, keys, values, window):
    row = lax.axis_index(ROW)
    mine = lax.axis_index("x")
    block = row * X + mine
    upper = lax.axis_index("y")
    in_plane = lax.axis_index("z")
    place = jnp.stack([row, mine, block, window[0], in_plane, upper]).astype(jnp.int32)

    own = jnp.concatenate([keys, values.T], axis=0)
    other = lax.ppermute(own, "y", [(0, 1)])
    kv = to_all(own, "z", PLANE)
    turned = queries.T
    all_q = [turned]
    for step in (1, 2, 3):
        all_q.append(lax.ppermute(turned, "x", [(i, (i + step) % X) for i in range(X)]))
    kv_other = to_all(other, "z", PLANE)
    acc, top, q_all = own_plane(place, all_q, kv)
    kv_other, top = lax.optimization_barrier((kv_other, top))

    def row_before(steps):
        same = lax.dynamic_index_in_dim(kv, jnp.maximum(in_plane - steps, 0), 0, keepdims=False)
        if steps == 0:
            return same
        crossed = lax.dynamic_index_in_dim(
            kv_other, (in_plane + PLANE - steps) % PLANE, 0, keepdims=False
        )
        return jnp.where(in_plane >= steps, same, crossed)

    near = to_all(jnp.concatenate([row_before(2), row_before(1), own], axis=0), "x", X)
    parts = other_plane(place, q_all, acc, top, kv_other)
    parts = lax.all_to_all(parts, "x", 0, 0, tiled=True)
    prob, out, kt, vw = student_forward(place, turned, near)
    grad, row_dot, squares = merge(parts, out)
    squares = jnp.sum(lax.all_to_all(squares, ("x", "yh", "core"), 0, 0, tiled=True), axis=0)
    grad_q, terms = student_backward(place, queries, prob, grad, row_dot, kt, vw)
    terms = lax.all_to_all(terms, "x", 0, 0, tiled=True)
    squares = jnp.sum(to_all(squares, ROW, ROWS), axis=0)
    loss = squares[0, 0] / (SEQ * QH * HD)

    sums = jnp.sum(terms.astype(jnp.float32), axis=0).reshape(3, 2 * HD, BLK)

    def back(value, steps):
        return lax.ppermute(
            value.astype(jnp.bfloat16), ROW, [(r, r - steps) for r in range(steps, ROWS)]
        )

    one = back(sums[1], 1)
    two = back(sums[0], 2)
    grads = sums[2] + one.astype(jnp.float32) + two.astype(jnp.float32)
    return (loss, grad_q, grads[:HD] * SCALE, grads[HD:])


def solution(mesh):
    finer = Mesh(mesh.devices.reshape(2, 8, 4, 4, 2), ("y", "z", "x", "yh", "core"))
    return jax.shard_map(
        step,
        mesh=finer,
        in_specs=(P(CTX, HEAD), P(CTX, HEAD), P(CTX, HEAD), P(HEAD)),
        out_specs=(P(), P(CTX, HEAD), P(CTX, HEAD), P(CTX, HEAD)),
        check_vma=False,
    )
```
